32 devices in a mesh: ctx: 16 (over z, y, core), wsh: 2 (over x).
Axes of the slice: x: 2, y: 2, z: 4, core: 2. Of those that a mesh axis runs over, the one named last changes fastest.
Arguments:
- tokens: bfloat16 [4096, 768], P(('ctx', 'wsh')), may hold values from -6 to 6
- lengths: int32 [8], replicated, may hold values from 1 to 2048, 4096 in all
- deal_order: int32 [32], replicated, may hold values from 0 to 31, each once
- w_qkv: bfloat16 [768, 2304], P('wsh'), may hold values from -0.21875 to 0.21875
- b_query: bfloat16 [768], P('wsh'), may hold values from -1 to 1
- b_value: bfloat16 [768], P('wsh'), may hold values from -1 to 1
- g_attn: bfloat16 [768], P('wsh'), may hold values from 0.3984375 to 1.59375
- c_attn: bfloat16 [768], P('wsh'), may hold values from -1 to 1
- w_out: bfloat16 [768, 768], P('wsh'), may hold values from -0.375 to 0.375
- b_out: bfloat16 [768], P('wsh'), may hold values from -1 to 1
- g_inner: bfloat16 [768], P('wsh'), may hold values from 0.3984375 to 1.59375
- c_inner: bfloat16 [768], P('wsh'), may hold values from -1 to 1
- w_up: bfloat16 [768, 3072], P('wsh'), may hold values from -0.21875 to 0.21875
- b_up: bfloat16 [3072], P('wsh'), may hold values from -1 to 1
- g_ffn: bfloat16 [768], P('wsh'), may hold values from 0.3984375 to 1.59375
- c_ffn: bfloat16 [768], P('wsh'), may hold values from -1 to 1
- w_down: bfloat16 [3072, 768], P('wsh'), may hold values from -0.1875 to 0.1875
- b_down: bfloat16 [768], P('wsh'), may hold values from -1 to 1
- g_mid: bfloat16 [3072], P('wsh'), may hold values from 0.3984375 to 1.59375
- c_mid: bfloat16 [3072], P('wsh'), may hold values from -1 to 1
- cotangent: bfloat16 [4096, 768], P(('ctx', 'wsh')), may hold values from -6 to 6
Outputs:
- layer_out: bfloat16 [4096, 768], P(('ctx', 'wsh'))
- grad_tokens: bfloat16 [4096, 768], P(('ctx', 'wsh'))
- lse_slots: float32 [12, 4096], P(None, ('ctx', 'wsh'))
- grad_w_qkv: float32 [768, 2304], P('wsh')
- grad_b_query: float32 [768], P('wsh')
- grad_b_value: float32 [768], P('wsh')
- grad_g_attn: float32 [768], P('wsh')
- grad_c_attn: float32 [768], P('wsh')
- grad_w_out: float32 [768, 768], P('wsh')
- grad_b_out: float32 [768], P('wsh')
- grad_g_inner: float32 [768], P('wsh')
- grad_c_inner: float32 [768], P('wsh')
- grad_w_up: float32 [768, 3072], P('wsh')
- grad_b_up: float32 [3072], P('wsh')
- grad_g_ffn: float32 [768], P('wsh')
- grad_c_ffn: float32 [768], P('wsh')
- grad_w_down: float32 [3072, 768], P('wsh')
- grad_b_down: float32 [768], P('wsh')
- grad_g_mid: float32 [3072], P('wsh')
- grad_c_mid: float32 [3072], P('wsh')
The draws below stay inside these ranges and needn't reach their ends.
Inputs may be any that keep to these rules, and one draw needn't show every extreme that they name: lengths of the 8 sequences in the given order; they sum to 4096 and the longest is exactly 2048. deal_order[g] is the slot of block g (rows g * 128 onward of the given order); slot s is on the device with index s // 1 of ctx+wsh, at its rows (s % 1) * 128 onward; each slot is used once.
All inputs are finite; a program needn't handle non-finite values.
Results may differ from the reference program's by a relative error of at most 0.02.
Values may be sent and summed in bfloat16 or wider, within the bound.
No kernel may reach another device: no remote copies, remote signals or barrier semaphores. Data moves between devices by JAX's collectives and lax.ppermute only.
A program may use at most 512 MiB of HBM per device.

```python
import math
from functools import partial
import jax
import jax.numpy as jnp
import numpy as np
from jax import lax

D = 768
HEADS = 12
HD = 64
FF = 3072
BLK = 128
NSEQ = 8
TOKENS = 4096
NBLK = 32
MAXLEN = 2048


def level_of(rng, shape, pieces, low, high):
    factor_of = 1.0
    for dim, blocks in pieces:
        draws = jax.random.uniform(jax.random.fold_in(jax.random.fold_in(rng, 6), dim), (blocks,), jnp.float32, low / len(pieces), high / len(pieces))
        factor_of = factor_of * jnp.repeat(jnp.exp(draws), shape[dim] // blocks).reshape((-1,) + (1,) * (len(shape) - 1 - dim))
    return factor_of


def length_profile(count, total, reach, lean):
    portions = [(1 << 20) // math.isqrt(rank ** lean) + 1 for rank in range(2, count + 1)]
    rest, given = total - reach - (count - 1), [1] * (count - 1)
    while rest > 0:
        movable = [i for i in range(count - 1) if given[i] < reach]
        mass, remaining = sum([portions[i] for i in movable]), rest
        for i in movable:
            addition = min(reach - given[i], max(1, remaining * portions[i] // mass), rest)
            given[i] = given[i] + addition
            rest = rest - addition
    return np.array([reach] + given)


def uneven_parts(own_key, amount, total, limit, slope):
    if amount == 2:
        one = jax.random.randint(own_key, (), max(1, total - limit), min(limit, total - 1) + 1)
        return jnp.stack([one, total - one])
    tallies = jnp.asarray(length_profile(amount, total, limit, slope), jnp.int32)
    couples = (amount - 1) // 2
    donor, taker = tallies[1:1 + 2 * couples:2], tallies[2:2 + 2 * couples:2]
    slack = jnp.minimum(donor - 1, limit - taker)
    passed = jax.random.randint(jax.random.fold_in(own_key, 1), (couples,), 0, 1 << 20) % (slack + 1)
    tallies = tallies.at[1:1 + 2 * couples:2].set(donor - passed).at[2:2 + 2 * couples:2].set(taker + passed)
    return tallies[jax.random.permutation(jax.random.fold_in(own_key, 2), amount)]


def scatter_about(own_key, shape, spread, limit, split=(), held_as=jnp.bfloat16):
    drawn = jax.random.normal(own_key, shape, jnp.float32) * spread
    if len(split) > 0:
        drawn = level_of(own_key, shape, split, -0.22, 0.18) * drawn
    return jnp.clip(drawn, min=-limit, max=limit).astype(held_as)


def setup_inputs(seed: int = 0) -> dict:
    key_list = jax.random.split(jax.random.key(seed), 22)
    tokens = scatter_about(key_list[0], (TOKENS, D), 1.0, 6.0, ((0, 32),))
    lengths = uneven_parts(key_list[1], NSEQ, TOKENS, MAXLEN, 2).astype(jnp.int32)
    deal_order = jax.random.permutation(key_list[2], NBLK).astype(jnp.int32)
    w_qkv = scatter_about(key_list[3], (D, 3 * D), D ** -0.5, 0.21875, ((0, 2),))
    b_query = scatter_about(key_list[4], (D,), 0.2, 1.0, ((0, 2),))
    b_value = scatter_about(key_list[5], (D,), 0.2, 1.0, ((0, 2),))
    g_attn = jnp.clip(1.0 + 0.12 * jax.random.normal(key_list[6], (D,), jnp.float32), 0.3984375, 1.59375).astype(jnp.bfloat16)
    c_attn = scatter_about(key_list[7], (D,), 0.2, 1.0, ((0, 2),))
    w_out = scatter_about(key_list[8], (D, D), (D * 100 // 318) ** -0.5, 0.375, ((0, 2),))
    b_out = scatter_about(key_list[9], (D,), 0.2, 1.0, ((0, 2),))
    g_inner = jnp.clip(1.0 + 0.12 * jax.random.normal(key_list[10], (D,), jnp.float32), 0.3984375, 1.59375).astype(jnp.bfloat16)
    c_inner = scatter_about(key_list[11], (D,), 0.2, 1.0, ((0, 2),))
    w_up = scatter_about(key_list[12], (D, FF), D ** -0.5, 0.21875, ((0, 2),))
    b_up = scatter_about(key_list[13], (FF,), 0.2, 1.0, ((0, 2),))
    g_ffn = jnp.clip(1.0 + 0.12 * jax.random.normal(key_list[14], (D,), jnp.float32), 0.3984375, 1.59375).astype(jnp.bfloat16)
    c_ffn = scatter_about(key_list[15], (D,), 0.2, 1.0, ((0, 2),))
    w_down = scatter_about(key_list[16], (FF, D), (FF * 100 // 318) ** -0.5, 0.1875, ((0, 2),))
    b_down = scatter_about(key_list[17], (D,), 0.2, 1.0, ((0, 2),))
    g_mid = jnp.clip(1.0 + 0.12 * jax.random.normal(key_list[18], (FF,), jnp.float32), 0.3984375, 1.59375).astype(jnp.bfloat16)
    c_mid = scatter_about(key_list[19], (FF,), 0.2, 1.0, ((0, 2),))
    cotangent = scatter_about(key_list[20], (TOKENS, D), 1.0, 6.0, ((0, 32),))
    return {"tokens": tokens, "lengths": lengths, "deal_order": deal_order, "w_qkv": w_qkv, "b_query": b_query, "b_value": b_value, "g_attn": g_attn, "c_attn": c_attn, "w_out": w_out, "b_out": b_out, "g_inner": g_inner, "c_inner": c_inner, "w_up": w_up, "b_up": b_up, "g_ffn": g_ffn, "c_ffn": c_ffn, "w_down": w_down, "b_down": b_down, "g_mid": g_mid, "c_mid": c_mid, "cotangent": cotangent}


@jax.custom_vjp
def low(v):
    return lax.optimization_barrier(v.astype(jnp.bfloat16)).astype(jnp.float32)

@jax.custom_vjp
def low_back(v):
    return v

def low_keep(v):
    return (low(v), None)

def low_pass(kept, grad):
    return (grad,)

def back_keep(v):
    return (v, None)

def back_low(kept, grad):
    return (low(grad),)
low.defvjp(low_keep, low_pass)
low_back.defvjp(back_keep, back_low)
EPSILON = 1e-05
SCALE = 0.125
NEG_FILL = -1e+30
HIGH = lax.Precision.HIGHEST

def layer_norm(values, gain_vec, shift_vec):
    center = values - lax.optimization_barrier(jnp.mean(values, axis=-1, keepdims=True))
    return center * lax.rsqrt(lax.optimization_barrier(jnp.mean(center * center, axis=-1, keepdims=True)) + EPSILON) * gain_vec + shift_vec

def product(left_mat, right_mat):
    return jnp.dot(left_mat, right_mat, precision=HIGH, preferred_element_type=jnp.float32)

def attend_block(query_blk, token_blk, segment_blk, keys_all, values_all, token_all, segment_all):
    scores = jnp.einsum('qhd,khd->hqk', query_blk, keys_all, precision=HIGH) * SCALE
    scores = low_back(scores)
    allowed = (segment_blk[:, None] == segment_all[None, :]) & (token_all[None, :] <= token_blk[:, None])
    scores = jnp.where(allowed[None], scores, NEG_FILL)
    top_score = lax.optimization_barrier(jnp.max(scores, axis=2, keepdims=True))
    shifted = jnp.exp(scores - top_score)
    totals = lax.optimization_barrier(jnp.sum(shifted, axis=2, keepdims=True))
    prob_low = low(shifted / totals)
    attended = jnp.einsum('hqk,khd->qhd', prob_low, values_all, precision=HIGH)
    log_total = top_score[:, :, 0] + jnp.log(totals[:, :, 0])
    return (attended, log_total)

def attention(query, keyvec, values, positions, segments):
    block_rows = min(512, TOKENS)
    count_blocks = TOKENS // block_rows

    def one_block(block_items):
        return jax.checkpoint(attend_block)(block_items[0], block_items[1], block_items[2], keyvec, values, positions, segments)
    results, log_totals = lax.map(one_block, (query.reshape(count_blocks, block_rows, HEADS, HD), positions.reshape(count_blocks, block_rows), segments.reshape(count_blocks, block_rows)))
    return (results.reshape(TOKENS, D), jnp.transpose(log_totals, (1, 0, 2)).reshape(HEADS, TOKENS))

def forward(positions, segments, tokens_f, w_qkv, b_query, b_value, g_attn, c_attn, w_out, b_out, g_inner, c_inner, w_up, b_up, g_ffn, c_ffn, w_down, b_down, g_mid, c_mid):
    attn_in = low(layer_norm(tokens_f, g_attn, c_attn))
    projected = product(attn_in, w_qkv)
    query = low(low_back(projected[:, :D] + b_query))
    keyvec = low(low_back(projected[:, D:2 * D]))
    values = low(low_back(projected[:, 2 * D:] + b_value))
    attended, log_totals = attention(query.reshape(TOKENS, HEADS, HD), keyvec.reshape(TOKENS, HEADS, HD), values.reshape(TOKENS, HEADS, HD), positions, segments)
    attended = low_back(attended)
    inner = low(layer_norm(attended, g_inner, c_inner))
    middle = tokens_f + low_back(product(inner, w_out) + b_out)
    ffn_in = low(layer_norm(middle, g_ffn, c_ffn))
    pre_act = low_back(product(ffn_in, w_up) + b_up)
    activated = jax.nn.gelu(pre_act, approximate=False)
    ffn_mid = low(layer_norm(activated, g_mid, c_mid))
    result = middle + low_back(product(ffn_mid, w_down) + b_down)
    return (result, log_totals)

def reference(tokens, lengths, deal_order, w_qkv, b_query, b_value, g_attn, c_attn, w_out, b_out, g_inner, c_inner, w_up, b_up, g_ffn, c_ffn, w_down, b_down, g_mid, c_mid, cotangent):
    positions = jnp.arange(TOKENS, dtype=jnp.int32)
    seq_ends = jnp.cumsum(lengths).astype(jnp.int32)
    segments = lax.optimization_barrier(jnp.sum((positions[:, None] >= seq_ends[None, :]).astype(jnp.int32), axis=1)).astype(jnp.int32)
    params = tuple((member.astype(jnp.float32) for member in (w_qkv, b_query, b_value, g_attn, c_attn, w_out, b_out, g_inner, c_inner, w_up, b_up, g_ffn, c_ffn, w_down, b_down, g_mid, c_mid)))
    layer_fn = partial(forward, positions, segments)
    result, pullback, log_totals = jax.vjp(layer_fn, tokens.astype(jnp.float32), *params, has_aux=True)
    grads = pullback(cotangent.astype(jnp.float32))
    inverse = jnp.zeros((NBLK,), jnp.int32).at[deal_order].set(jnp.arange(NBLK, dtype=jnp.int32))
    slot_ids = jnp.arange(TOKENS, dtype=jnp.int32)
    source = inverse[slot_ids // BLK] * BLK + slot_ids % BLK
    lse_slots = log_totals[:, source]
    return (result.astype(jnp.bfloat16), grads[0].astype(jnp.bfloat16), lse_slots, grads[1], grads[2], grads[3], grads[4], grads[5], grads[6], grads[7], grads[8], grads[9], grads[10], grads[11], grads[12], grads[13], grads[14], grads[15], grads[16], grads[17])
```

```python
from functools import partial

import jax
import jax.numpy as jnp
from jax import lax
from jax.experimental import pallas as pl
from jax.experimental.pallas import tpu as pltpu
from jax.sharding import Mesh, PartitionSpec as P

HEADS = 12
BLK = 128
HD = 64
TILE = 256
KEYS = 512

EPSILON = 1e-05
SCALE = 0.125
NEG_FILL = -1e30
ALL = ("hi", "core", "wsh")
CHIPS = ("hi", "wsh")
BF = jnp.bfloat16
F32 = jnp.float32


def layer_norm(values, gain_vec, shift_vec):
    center = values - jnp.mean(values, axis=-1, keepdims=True)
    return (
        center * lax.rsqrt(jnp.mean(center * center, axis=-1, keepdims=True) + EPSILON) * gain_vec
        + shift_vec
    )


def swap(value, axis):
    return lax.ppermute(value, axis, [(0, 1), (1, 0)])


def in_order(flag, first, second, axis=0):
    return jnp.where(
        flag == 0,
        jnp.concatenate([first, second], axis=axis),
        jnp.concatenate([second, first], axis=axis),
    )


def nt_dot(left, right):
    return lax.dot_general(left, right, (((1,), (1,)), ((), ())), preferred_element_type=F32)


def unpack_rows(packed, upper):
    lane = lax.broadcasted_iota(jnp.int32, (HD, BLK), 1)
    pick = (lane >= HD) if upper else (lane < HD)
    rows = []
    for block in range(2):
        value = packed[block].astype(F32)
        rolled = pltpu.roll(value, HD, 1)
        first, second = (rolled, value) if upper else (value, rolled)
        rows += [jnp.where(pick, first, 0.0), jnp.where(pick, second, 0.0)]
    return jnp.concatenate(rows, axis=0)


def pack_rows(wide, upper):
    lane = lax.broadcasted_iota(jnp.int32, (HD, BLK), 1)
    out = []
    for block in range(2):
        first = wide[block * BLK : block * BLK + HD]
        second = wide[block * BLK + HD : (block + 1) * BLK]
        if upper:
            first = pltpu.roll(first, HD, 1)
        else:
            second = pltpu.roll(second, HD, 1)
        out.append(jnp.where(lane < HD, first, second))
    return out


def seen(chunk, qpos, start):
    kpos = chunk * KEYS + lax.broadcasted_iota(jnp.int32, (KEYS, TILE), 0)
    return (kpos >= start) & (kpos <= qpos)


def forward_kernel(table, q_ref, kv_ref, kvt_ref, start_ref, packed_ref, out_ref, lse_ref):
    tile = pl.program_id(0)
    query = (unpack_rows(q_ref[0], False) * SCALE).astype(BF)
    start = start_ref[0]
    qpos = table[0, tile] + lax.broadcasted_iota(jnp.int32, (1, TILE), 1)

    def step(chunk, carry):
        top, total, acc = carry
        at = pl.multiple_of(chunk * KEYS, KEYS)
        scores = nt_dot(kv_ref[pl.ds(at, KEYS), :], query)
        scores = jnp.where(seen(chunk, qpos, start), scores, NEG_FILL)
        new_top = jnp.maximum(top, jnp.max(scores, axis=0, keepdims=True))
        weights = jnp.exp(scores - new_top)
        factor = jnp.exp(top - new_top)
        added = jnp.dot(
            kvt_ref[:, pl.ds(at, KEYS)], weights.astype(BF), preferred_element_type=F32
        )
        return (
            new_top,
            total * factor + jnp.sum(weights, axis=0, keepdims=True),
            acc * factor + added,
        )

    top, total, acc = lax.fori_loop(
        table[1, tile],
        table[2, tile],
        step,
        (
            jnp.full((1, TILE), NEG_FILL, F32),
            jnp.zeros((1, TILE), F32),
            jnp.zeros((BLK, TILE), F32),
        ),
    )
    out_t = acc / total
    out_ref[0] = out_t
    lse_ref[0] = top + jnp.log(total)
    first, second = pack_rows(jnp.transpose(out_t), True)
    packed_ref[0, 0] = first.astype(BF)
    packed_ref[0, 1] = second.astype(BF)


def backward_kernel(
    table, q_ref, do_ref, kv_ref, kvt_ref, start_ref, out_ref, lse_ref, dq_ref, dkv_ref, sum_ref
):
    tile = pl.program_id(0)

    @pl.when(tile == 0)
    def _():
        sum_ref[...] = jnp.zeros_like(sum_ref)

    query = (unpack_rows(q_ref[0], False) * SCALE).astype(BF)
    dout_f = unpack_rows(do_ref[0], True)
    dout = dout_f.astype(BF)
    delta = jnp.sum(jnp.transpose(dout_f) * out_ref[0], axis=0, keepdims=True)
    both = jnp.concatenate([query, dout], axis=0)
    start = start_ref[0]
    lse = lse_ref[0]
    qpos = table[0, tile] + lax.broadcasted_iota(jnp.int32, (1, TILE), 1)

    def step(chunk, dq_t):
        at = pl.multiple_of(chunk * KEYS, KEYS)
        kv = kv_ref[pl.ds(at, KEYS), :]
        scores = nt_dot(kv, query)
        probs = jnp.where(seen(chunk, qpos, start), jnp.exp(scores - lse), 0.0)
        dscore = (probs * (nt_dot(kv, dout) - delta)).astype(BF)
        pair = jnp.concatenate([dscore, probs.astype(BF)], axis=1)
        sum_ref[pl.ds(at, KEYS), :] += jnp.dot(pair, both, preferred_element_type=F32)
        return dq_t + jnp.dot(kvt_ref[:, pl.ds(at, KEYS)], dscore, preferred_element_type=F32)

    dq_t = lax.fori_loop(table[1, tile], table[2, tile], step, jnp.zeros((BLK, TILE), F32))
    first, second = pack_rows(jnp.transpose(dq_t) * SCALE, False)
    dq_ref[0, 0] = first.astype(BF)
    dq_ref[0, 1] = second.astype(BF)

    @pl.when(tile == pl.num_programs(0) - 1)
    def _():
        dkv_ref[...] = sum_ref[...].astype(BF)


def spec(*shape):
    return pl.BlockSpec((1,) + shape, lambda i, table: (i,) + (0,) * len(shape))


def whole(*shape):
    return pl.BlockSpec(
        shape, lambda i, table: (0,) * len(shape), pipeline_mode=pl.Buffered(1)
    )


def attend_forward(table, queries, kv, kvt, starts):
    tiles = queries.shape[0]
    keys = kv.shape[0]
    return pl.pallas_call(
        forward_kernel,
        name="attend_forward",
        grid_spec=pltpu.PrefetchScalarGridSpec(
            num_scalar_prefetch=1,
            grid=(tiles,),
            in_specs=[spec(2, HD, BLK), whole(keys, BLK), whole(BLK, keys), spec(1, TILE)],
            out_specs=[spec(2, HD, BLK), spec(BLK, TILE), spec(1, TILE)],
        ),
        out_shape=[
            jax.ShapeDtypeStruct((tiles, 2, HD, BLK), BF),
            jax.ShapeDtypeStruct((tiles, BLK, TILE), F32),
            jax.ShapeDtypeStruct((tiles, 1, TILE), F32),
        ],
    )(table, queries, kv, kvt, starts)


def attend_backward(table, queries, douts, kv, kvt, starts, out_t, lse):
    tiles = queries.shape[0]
    keys = kv.shape[0]
    return pl.pallas_call(
        backward_kernel,
        name="attend_backward",
        grid_spec=pltpu.PrefetchScalarGridSpec(
            num_scalar_prefetch=1,
            grid=(tiles,),
            in_specs=[
                spec(2, HD, BLK),
                spec(2, HD, BLK),
                whole(keys, BLK),
                whole(BLK, keys),
                spec(1, TILE),
                spec(BLK, TILE),
                spec(1, TILE),
            ],
            out_specs=[
                spec(2, HD, BLK),
                pl.BlockSpec((keys, BLK), lambda i, table: (0, 0)),
            ],
            scratch_shapes=[pltpu.VMEM((keys, BLK), F32)],
        ),
        out_shape=[
            jax.ShapeDtypeStruct((tiles, 2, HD, BLK), BF),
            jax.ShapeDtypeStruct((keys, BLK), BF),
        ],
    )(table, queries, douts, kv, kvt, starts, out_t, lse)


def partner(axis, bit, size):
    return [(i, i ^ bit) for i in range(size)]


def reduce_steps(value, order, sizes, index):
    for axis, bit in order:
        half = value.shape[0] // 2
        mine = (index[axis] // bit) % 2
        kept = lax.dynamic_slice_in_dim(value, mine * half, half, 0)
        sent = lax.dynamic_slice_in_dim(value, (1 - mine) * half, half, 0)
        got = lax.ppermute(sent, axis, partner(axis, bit, sizes[axis]))
        value = (kept.astype(F32) + got.astype(F32)).astype(value.dtype)
    return value


def gather_steps(value, order, sizes, index):
    for axis, bit in reversed(order):
        mine = (index[axis] // bit) % 2
        got = lax.ppermute(value, axis, partner(axis, bit, sizes[axis]))
        value = in_order(mine, value, got)
    return value


def sum_over_ctx(value, order, sizes, index):
    rows = value.shape[0]
    count = sizes["hi"] * 2
    parts = value.reshape((count, rows // count) + value.shape[1:])
    parts = reduce_steps(parts, order, sizes, index)
    parts = gather_steps(parts, order, sizes, index)
    return parts.reshape(value.shape).astype(F32)


def body(
    hi_size,
    tokens,
    lengths,
    deal_order,
    w_qkv,
    b_query,
    b_value,
    g_attn,
    c_attn,
    w_out,
    b_out,
    g_inner,
    c_inner,
    w_up,
    b_up,
    g_ffn,
    c_ffn,
    w_down,
    b_down,
    g_mid,
    c_mid,
    cotangent,
):
    rows, feature = tokens.shape
    hidden = w_down.shape[0] * 2
    chips = hi_size * 2
    hi = lax.axis_index("hi")
    core = lax.axis_index("core")
    wsh = lax.axis_index("wsh")
    sizes = {"hi": hi_size, "core": 2}
    index = {"hi": hi, "core": core}
    bits = []
    while 2 ** len(bits) < hi_size:
        bits.append(2 ** len(bits))
    plain = [("core", 1)] + [("hi", bit) for bit in bits]
    turned = [("core", 1)] + [("hi", bit) for bit in bits[1:] + bits[:1]]

    total = hi_size * 4 * BLK
    seq_ends = jnp.cumsum(lengths)
    qbase = (jnp.arange(hi_size, dtype=jnp.int32) * 4 + core * 2) * BLK
    qpos = qbase[:, None] + jnp.arange(TILE, dtype=jnp.int32)[None, :]
    starts = jnp.max(
        jnp.where(seq_ends[None, None, :] <= qpos[:, :, None], seq_ends[None, None, :], 0), axis=2
    ).astype(jnp.int32)
    table = jnp.stack([qbase, starts[:, 0] // KEYS, (qbase + TILE - 1) // KEYS + 1]).astype(
        jnp.int32
    )
    starts = starts[:, None, :]

    small = [b_query, b_value, g_attn, c_attn, b_out, g_inner, c_inner, g_ffn, c_ffn, b_down]
    large = [b_up, g_mid, c_mid]
    vec = jnp.concatenate(small + large).reshape(-1, BLK)
    vec_got = swap(vec, "wsh").reshape(-1)
    vectors = []
    at = 0
    for member in small + large:
        size = member.shape[0]
        vectors.append(in_order(wsh, member, vec_got[at : at + size]).astype(F32))
        at += size
    (bq, bv, ga, ca, bo, gi, ci, gf, cf, bd, bu, gm, cm) = vectors

    def whole_weight(weight, after):
        if after is not None:
            weight, _ = lax.optimization_barrier((weight, after))
        half = weight.shape[0] // 2
        sent = lax.dynamic_slice_in_dim(weight, core * half, half, 0)
        first = swap(sent, "wsh")
        second = swap(first, "core")
        return in_order(wsh, weight, in_order(core, first, second)), first

    qkv_full, mark = whole_weight(w_qkv, None)
    out_full, mark = whole_weight(w_out, mark)
    up_full, mark = whole_weight(w_up, mark)
    down_full, mark = whole_weight(w_down, mark)
    cot_pair = swap(lax.optimization_barrier((cotangent, mark))[0], "wsh")

    inputs = tokens.astype(F32)
    normed_attn, back_attn = jax.vjp(layer_norm, inputs, ga, ca)
    attn_low = normed_attn.astype(BF)
    projected = jnp.dot(attn_low, qkv_full, preferred_element_type=F32)
    query_low = (projected[:, :feature] + bq).astype(BF)
    key_low = projected[:, feature : 2 * feature].astype(BF)
    value_low = (projected[:, 2 * feature :] + bv).astype(BF)

    def side_by_side(value):
        split = value.reshape(2, HD, HEADS, HD)
        return jnp.transpose(split, (2, 1, 0, 3)).reshape(HEADS, HD, BLK)

    def back_to_rows(value):
        split = value.reshape(HEADS, HD, 2, HD)
        return jnp.transpose(split, (2, 1, 0, 3)).reshape(rows, feature)

    def to_heads(value):
        padded = jnp.pad(value, ((0, chips - HEADS), (0, 0), (0, 0)))
        return lax.all_to_all(padded, CHIPS, 0, 0, tiled=True)

    def to_tokens(value):
        return lax.all_to_all(value, CHIPS, 0, 0, tiled=True)[:HEADS]

    kv_low = jnp.concatenate(
        [key_low.reshape(rows, HEADS, HD), value_low.reshape(rows, HEADS, HD)], axis=2
    )
    kv_low = jnp.transpose(kv_low, (1, 0, 2))
    message = to_heads(jnp.concatenate([kv_low, side_by_side(query_low)], axis=1))
    kv_mine = message[:, :BLK].reshape(hi_size, 1, 2 * BLK, BLK)
    queries = message[:, BLK:].reshape(hi_size, 2, HD, BLK)
    kv_all = in_order(core, kv_mine, swap(kv_mine, "core"), axis=1).reshape(total, BLK)
    kv_turned = jnp.transpose(kv_all)
    packed, out_t, lse = attend_forward(table, queries, kv_all, kv_turned, starts)
    attended = back_to_rows(to_tokens(packed.reshape(chips, HD, BLK))).astype(F32)

    lse_all = lax.all_gather(lse.reshape(chips, BLK), ALL, axis=0, tiled=True)
    slot = hi * 4 + core * 2 + wsh
    given = jnp.sum(
        jnp.where(deal_order == slot, jnp.arange(deal_order.shape[0], dtype=jnp.int32), 0)
    )
    lse_all = lse_all.reshape(hi_size, 2, 2, chips, BLK)
    lse_all = lax.dynamic_index_in_dim(lse_all, (given // 2) % 2, 1, keepdims=False)
    lse_all = lax.dynamic_index_in_dim(
        lse_all, (given // 4) * 2 + given % 2, 2, keepdims=False
    )
    lse_slots = lse_all.reshape(chips, BLK)[:HEADS]

    normed_inner, back_inner = jax.vjp(layer_norm, attended, gi, ci)
    inner_low = normed_inner.astype(BF)
    middle = inputs + jnp.dot(inner_low, out_full, preferred_element_type=F32) + bo
    normed_ffn, back_ffn = jax.vjp(layer_norm, middle, gf, cf)
    ffn_low = normed_ffn.astype(BF)
    pre_act = jnp.dot(ffn_low, up_full, preferred_element_type=F32) + bu
    activated, back_gelu = jax.vjp(partial(jax.nn.gelu, approximate=False), pre_act)
    normed_mid, back_mid = jax.vjp(layer_norm, activated, gm, cm)
    mid_low = normed_mid.astype(BF)
    layer_low = (middle + jnp.dot(mid_low, down_full, preferred_element_type=F32) + bd).astype(BF)

    d_out_f = cotangent.astype(F32)
    grad_bd = jnp.sum(d_out_f, axis=0)
    d_mid, grad_gm, grad_cm = back_mid(
        jnp.einsum("tj,ij->ti", cotangent, down_full, preferred_element_type=F32)
    )
    d_pre = back_gelu(d_mid)[0].astype(BF)
    grad_bu = jnp.sum(d_pre.astype(F32), axis=0)
    d_ffn, grad_gf, grad_cf = back_ffn(
        jnp.einsum("tj,ij->ti", d_pre, up_full, preferred_element_type=F32)
    )
    d_middle = d_out_f + d_ffn
    d_branch = d_middle.astype(BF)
    grad_bo = jnp.sum(d_branch.astype(F32), axis=0)
    d_att, grad_gi, grad_ci = back_inner(
        jnp.einsum("tj,ij->ti", d_branch, out_full, preferred_element_type=F32)
    )
    d_att_low = d_att.astype(BF)

    def halves(value):
        size = value.shape[1] // 2
        mine = lax.dynamic_slice_in_dim(value, wsh * size, size, 1)
        other = lax.dynamic_slice_in_dim(value, (1 - wsh) * size, size, 1)
        return mine, other

    def weight_grad(mine, got, right, right_got):
        left = jnp.concatenate([mine, got], axis=0)
        return jnp.einsum(
            "ti,tj->ij", left, jnp.concatenate([right, right_got], axis=0),
            preferred_element_type=F32,
        ).astype(BF)

    mid_mine, mid_other = halves(mid_low)
    ffn_mine, ffn_other = halves(ffn_low)
    inner_mine, inner_other = halves(inner_low)
    attn_mine, attn_other = halves(attn_low)
    mid_got = swap(mid_other, "wsh")
    acts_got = swap(jnp.concatenate([ffn_other, inner_other, attn_other], axis=1), "wsh")
    ffn_got, inner_got, attn_got = jnp.split(acts_got, 3, axis=1)
    pre_got = swap(d_pre, "wsh")
    branch_got = swap(d_branch, "wsh")
    grad_down = weight_grad(mid_mine, mid_got, cotangent, cot_pair)
    grad_up = weight_grad(ffn_mine, ffn_got, d_pre, pre_got)
    grad_out = weight_grad(inner_mine, inner_got, d_branch, branch_got)
    t_down = sum_over_ctx(grad_down, plain, sizes, index)
    t_up = sum_over_ctx(grad_up, turned, sizes, index)
    t_out = sum_over_ctx(grad_out, plain, sizes, index)

    douts = to_heads(side_by_side(d_att_low)).reshape(hi_size, 2, HD, BLK)
    dq_packed, dkv = attend_backward(
        table, queries, douts, kv_all, kv_turned, starts, out_t, lse
    )
    dkv = dkv.reshape(hi_size, 2, 2 * BLK, BLK)
    dkv_mine = lax.dynamic_index_in_dim(dkv, core, 1, keepdims=False)
    dkv_other = lax.dynamic_index_in_dim(dkv, 1 - core, 1, keepdims=False)
    dkv_sum = (dkv_mine.astype(F32) + swap(dkv_other, "core").astype(F32)).astype(BF)
    message = to_tokens(
        jnp.concatenate(
            [dkv_sum.reshape(chips, BLK, BLK), dq_packed.reshape(chips, HD, BLK)], axis=1
        )
    )
    dq_low = back_to_rows(message[:, BLK:])
    dkv_rows = jnp.transpose(message[:, :BLK], (1, 0, 2)).reshape(rows, HEADS, 2, HD)
    dk_low = dkv_rows[:, :, 0].reshape(rows, feature)
    dv_low = dkv_rows[:, :, 1].reshape(rows, feature)
    d_qkv = jnp.concatenate([dq_low, dk_low, dv_low], axis=1)
    d_got = swap(d_qkv, "wsh")
    grad_bq = jnp.sum(dq_low.astype(F32), axis=0)
    grad_bv = jnp.sum(dv_low.astype(F32), axis=0)
    d_input, grad_ga, grad_ca = back_attn(
        jnp.einsum("tj,ij->ti", d_qkv, qkv_full, preferred_element_type=F32)
    )
    grad_low = (d_middle + d_input).astype(BF)
    t_qkv = sum_over_ctx(
        weight_grad(attn_mine, attn_got, d_qkv, d_got), plain, sizes, index
    )

    grads = [
        grad_bq, grad_bv, grad_ga, grad_ca, grad_bo, grad_gi, grad_ci, grad_gf, grad_cf, grad_bd,
        grad_bu, grad_gm, grad_cm,
    ]
    mine_vec, other_vec = [], []
    for member in grads:
        mine, other = halves(member.reshape(1, -1))
        mine_vec.append(mine[0])
        other_vec.append(other[0])
    mine_vec = jnp.concatenate(mine_vec)
    length = mine_vec.shape[0]
    unit = hi_size * 2 * 8 * BLK
    padding = -length % unit
    mine_vec = jnp.pad(mine_vec, (0, padding)).reshape(hi_size * 2, -1, BLK)
    other_vec = jnp.pad(jnp.concatenate(other_vec), (0, padding)).reshape(hi_size * 2, -1, BLK)
    summed = mine_vec + swap(other_vec, "wsh")
    summed = reduce_steps(summed, plain, sizes, index)
    summed = gather_steps(summed, plain, sizes, index).reshape(-1)
    outs = []
    at = 0
    for member in small + large:
        outs.append(summed[at : at + member.shape[0]])
        at += member.shape[0]
    (t_bq, t_bv, t_ga, t_ca, t_bo, t_gi, t_ci, t_gf, t_cf, t_bd, t_bu, t_gm, t_cm) = outs
    return (
        layer_low,
        grad_low,
        lse_slots,
        t_qkv,
        t_bq,
        t_bv,
        t_ga,
        t_ca,
        t_out,
        t_bo,
        t_gi,
        t_ci,
        t_up,
        t_bu,
        t_gf,
        t_cf,
        t_down,
        t_bd,
        t_gm,
        t_cm,
    )


def solution(mesh):
    hi_size = mesh.shape["ctx"] // 2
    inner = Mesh(mesh.devices.reshape(hi_size, 2, mesh.shape["wsh"]), ALL)
    row, mat, vec = P(ALL, None), P("wsh", None), P("wsh")
    grads = (
        mat, vec, vec, vec, vec, mat, vec, vec, vec, mat, vec, vec, vec, mat, vec, vec, vec,
    )
    return jax.shard_map(
        partial(body, hi_size),
        mesh=inner,
        in_specs=(row, P(), P()) + grads + (row,),
        out_specs=(row, row, P(None, ALL)) + grads,
        check_vma=False,
    )
```

```python
from functools import partial

import jax
import jax.numpy as jnp
from jax import lax
from jax.experimental import pallas as pl
from jax.experimental.pallas import tpu as pltpu
from jax.sharding import Mesh, PartitionSpec as P

HEADS = 12
BLK = 128
HD = 64
TILE = 256
KEYS = 512

EPSILON = 1e-05
SCALE = 0.125
NEG_FILL = -1e30
ALL = ("hi", "core", "wsh")
CHIPS = ("hi", "wsh")
BF = jnp.bfloat16
F32 = jnp.float32


def layer_norm(values, gain_vec, shift_vec):
    center = values - jnp.mean(values, axis=-1, keepdims=True)
    return (
        center * lax.rsqrt(jnp.mean(center * center, axis=-1, keepdims=True) + EPSILON) * gain_vec
        + shift_vec
    )


def swap(value, axis):
    return lax.ppermute(value, axis, [(0, 1), (1, 0)])


def in_order(flag, first, second, axis=0):
    return jnp.where(
        flag == 0,
        jnp.concatenate([first, second], axis=axis),
        jnp.concatenate([second, first], axis=axis),
    )


def stacked(members):
    row = lax.broadcasted_iota(jnp.int32, (len(members), members[0].shape[0]), 0)
    value = jnp.broadcast_to(members[0][None, :], row.shape)
    for i in range(1, len(members)):
        value = jnp.where(row == i, members[i][None, :], value)
    return value


def nt_dot(left, right):
    return lax.dot_general(left, right, (((1,), (1,)), ((), ())), preferred_element_type=F32)


def unpack_rows(packed, upper):
    lane = lax.broadcasted_iota(jnp.int32, (HD, BLK), 1)
    pick = (lane >= HD) if upper else (lane < HD)
    rows = []
    for block in range(2):
        value = packed[block].astype(F32)
        rolled = pltpu.roll(value, HD, 1)
        first, second = (rolled, value) if upper else (value, rolled)
        rows += [jnp.where(pick, first, 0.0), jnp.where(pick, second, 0.0)]
    return jnp.concatenate(rows, axis=0)


def pack_rows(wide, upper):
    lane = lax.broadcasted_iota(jnp.int32, (HD, BLK), 1)
    out = []
    for block in range(2):
        first = wide[block * BLK : block * BLK + HD]
        second = wide[block * BLK + HD : (block + 1) * BLK]
        if upper:
            first = pltpu.roll(first, HD, 1)
        else:
            second = pltpu.roll(second, HD, 1)
        out.append(jnp.where(lane < HD, first, second))
    return out


def seen(chunk, shift, qpos, start):
    row = lax.broadcasted_iota(jnp.int32, (KEYS, TILE), 0)
    kpos = chunk * KEYS + ((row + shift) & (KEYS - 1))
    return (kpos >= start) & (kpos <= qpos)


def forward_kernel(
    table, q_ref, mine_ref, other_ref, start_ref, packed_ref, out_ref, lse_ref, kvt_ref
):
    tile = pl.program_id(0)

    @pl.when(tile == 0)
    def _():
        def turn(chunk, carry):
            kvt_ref[chunk, :, :TILE] = jnp.transpose(mine_ref[chunk].astype(F32)).astype(BF)
            kvt_ref[chunk, :, TILE:] = jnp.transpose(other_ref[chunk].astype(F32)).astype(BF)
            return carry

        lax.fori_loop(0, pl.num_programs(0), turn, 0)

    query = (unpack_rows(q_ref[0], False) * SCALE).astype(BF)
    start = start_ref[0]
    qpos = table[0, tile] + lax.broadcasted_iota(jnp.int32, (1, TILE), 1)
    shift = table[3, tile]

    def step(chunk, carry):
        top, total, acc = carry
        kv = jnp.concatenate([mine_ref[chunk], other_ref[chunk]], axis=0)
        scores = jnp.where(seen(chunk, shift, qpos, start), nt_dot(kv, query), NEG_FILL)
        new_top = jnp.maximum(top, jnp.max(scores, axis=0, keepdims=True))
        weights = jnp.exp(scores - new_top)
        factor = jnp.exp(top - new_top)
        added = jnp.dot(kvt_ref[chunk], weights.astype(BF), preferred_element_type=F32)
        return (
            new_top,
            total * factor + jnp.sum(weights, axis=0, keepdims=True),
            acc * factor + added,
        )

    top, total, acc = lax.fori_loop(
        table[1, tile],
        table[2, tile],
        step,
        (
            jnp.full((1, TILE), NEG_FILL, F32),
            jnp.zeros((1, TILE), F32),
            jnp.zeros((BLK, TILE), F32),
        ),
    )
    out_t = acc / total
    out_ref[0] = out_t
    lse_ref[0] = top + jnp.log(total)
    first, second = pack_rows(jnp.transpose(out_t), True)
    packed_ref[0, 0] = first.astype(BF)
    packed_ref[0, 1] = second.astype(BF)


def backward_kernel(
    table,
    q_ref,
    do_ref,
    mine_ref,
    other_ref,
    kvt_ref,
    start_ref,
    out_ref,
    lse_ref,
    dq_ref,
    wide_ref,
    dmine_ref,
    dother_ref,
    sum_ref,
):
    tile = pl.program_id(0)

    @pl.when(tile == 0)
    def _():
        sum_ref[...] = jnp.zeros_like(sum_ref)

    query = (unpack_rows(q_ref[0], False) * SCALE).astype(BF)
    dout_f = unpack_rows(do_ref[0], True)
    dout = dout_f.astype(BF)
    delta = jnp.sum(jnp.transpose(dout_f) * out_ref[0], axis=0, keepdims=True)
    both = jnp.concatenate([query, dout], axis=0)
    start = start_ref[0]
    lse = lse_ref[0]
    qpos = table[0, tile] + lax.broadcasted_iota(jnp.int32, (1, TILE), 1)
    shift = table[3, tile]

    def step(chunk, dq_t):
        kv = jnp.concatenate([mine_ref[chunk], other_ref[chunk]], axis=0)
        scores = nt_dot(kv, query)
        probs = jnp.where(seen(chunk, shift, qpos, start), jnp.exp(scores - lse), 0.0)
        dscore = (probs * (nt_dot(kv, dout) - delta)).astype(BF)
        pair = jnp.concatenate([dscore, probs.astype(BF)], axis=1)
        sum_ref[chunk] += jnp.dot(pair, both, preferred_element_type=F32)
        return dq_t + jnp.dot(kvt_ref[chunk], dscore, preferred_element_type=F32)

    dq_t = lax.fori_loop(table[1, tile], table[2, tile], step, jnp.zeros((BLK, TILE), F32))
    dq = jnp.transpose(dq_t) * SCALE
    lane = lax.broadcasted_iota(jnp.int32, (TILE, BLK), 1)
    wide_ref[0] = jnp.where(lane < HD, dq, 0.0).astype(BF)
    first, second = pack_rows(dq, False)
    dq_ref[0, 0] = first.astype(BF)
    dq_ref[0, 1] = second.astype(BF)

    @pl.when(tile == pl.num_programs(0) - 1)
    def _():
        dmine_ref[...] = sum_ref[:, :TILE].astype(BF)
        dother_ref[...] = sum_ref[:, TILE:].astype(BF)


def spec(*shape):
    return pl.BlockSpec((1,) + shape, lambda i, table: (i,) + (0,) * len(shape))


def whole(*shape):
    return pl.BlockSpec(
        shape, lambda i, table: (0,) * len(shape), pipeline_mode=pl.Buffered(1)
    )


def kept(*shape):
    return pl.BlockSpec(shape, lambda i, table: (0,) * len(shape))


def attend_forward(table, queries, mine, other, starts):
    tiles = queries.shape[0]
    return pl.pallas_call(
        forward_kernel,
        name="attend_forward",
        grid_spec=pltpu.PrefetchScalarGridSpec(
            num_scalar_prefetch=1,
            grid=(tiles,),
            in_specs=[
                spec(2, HD, BLK),
                whole(tiles, TILE, BLK),
                whole(tiles, TILE, BLK),
                spec(1, TILE),
            ],
            out_specs=[
                spec(2, HD, BLK),
                spec(BLK, TILE),
                spec(1, TILE),
                kept(tiles, BLK, KEYS),
            ],
        ),
        out_shape=[
            jax.ShapeDtypeStruct((tiles, 2, HD, BLK), BF),
            jax.ShapeDtypeStruct((tiles, BLK, TILE), F32),
            jax.ShapeDtypeStruct((tiles, 1, TILE), F32),
            jax.ShapeDtypeStruct((tiles, BLK, KEYS), BF),
        ],
    )(table, queries, mine, other, starts)


def attend_backward(table, queries, douts, mine, other, turned, starts, out_t, lse):
    tiles = queries.shape[0]
    return pl.pallas_call(
        backward_kernel,
        name="attend_backward",
        grid_spec=pltpu.PrefetchScalarGridSpec(
            num_scalar_prefetch=1,
            grid=(tiles,),
            in_specs=[
                spec(2, HD, BLK),
                spec(2, HD, BLK),
                whole(tiles, TILE, BLK),
                whole(tiles, TILE, BLK),
                whole(tiles, BLK, KEYS),
                spec(1, TILE),
                spec(BLK, TILE),
                spec(1, TILE),
            ],
            out_specs=[
                spec(2, HD, BLK),
                spec(TILE, BLK),
                kept(tiles, TILE, BLK),
                kept(tiles, TILE, BLK),
            ],
            scratch_shapes=[pltpu.VMEM((tiles, KEYS, BLK), F32)],
        ),
        out_shape=[
            jax.ShapeDtypeStruct((tiles, 2, HD, BLK), BF),
            jax.ShapeDtypeStruct((tiles, TILE, BLK), BF),
            jax.ShapeDtypeStruct((tiles, TILE, BLK), BF),
            jax.ShapeDtypeStruct((tiles, TILE, BLK), BF),
        ],
    )(table, queries, douts, mine, other, turned, starts, out_t, lse)


def partner(axis, bit, size):
    return [(i, i ^ bit) for i in range(size)]


def reduce_steps(value, order, sizes, index):
    for axis, bit in order:
        half = value.shape[0] // 2
        mine = (index[axis] // bit) % 2
        kept = lax.dynamic_slice_in_dim(value, mine * half, half, 0)
        sent = lax.dynamic_slice_in_dim(value, (1 - mine) * half, half, 0)
        got = lax.ppermute(sent, axis, partner(axis, bit, sizes[axis]))
        value = (kept.astype(F32) + got.astype(F32)).astype(value.dtype)
    return value


def gather_steps(value, order, sizes, index):
    for axis, bit in reversed(order):
        mine = (index[axis] // bit) % 2
        got = lax.ppermute(value, axis, partner(axis, bit, sizes[axis]))
        value = in_order(mine, value, got)
    return value


def sum_over_ctx(value, order, sizes, index):
    rows = value.shape[0]
    count = sizes["hi"] * 2
    parts = value.reshape((count, rows // count) + value.shape[1:])
    parts = reduce_steps(parts, order, sizes, index)
    parts = gather_steps(parts, order, sizes, index)
    return parts.reshape(value.shape).astype(F32)


def body(
    hi_size,
    tokens,
    lengths,
    deal_order,
    w_qkv,
    b_query,
    b_value,
    g_attn,
    c_attn,
    w_out,
    b_out,
    g_inner,
    c_inner,
    w_up,
    b_up,
    g_ffn,
    c_ffn,
    w_down,
    b_down,
    g_mid,
    c_mid,
    cotangent,
):
    rows, feature = tokens.shape
    hidden = w_down.shape[0] * 2
    chips = hi_size * 2
    hi = lax.axis_index("hi")
    core = lax.axis_index("core")
    wsh = lax.axis_index("wsh")
    sizes = {"hi": hi_size, "core": 2}
    index = {"hi": hi, "core": core}
    bits = []
    while 2 ** len(bits) < hi_size:
        bits.append(2 ** len(bits))
    plain = [("core", 1)] + [("hi", bit) for bit in bits]

    seq_ends = jnp.cumsum(lengths)
    qbase = (jnp.arange(hi_size, dtype=jnp.int32) * 4 + core * 2) * BLK
    qpos = qbase[:, None] + jnp.arange(TILE, dtype=jnp.int32)[None, :]
    starts = jnp.max(
        jnp.where(seq_ends[None, None, :] <= qpos[:, :, None], seq_ends[None, None, :], 0), axis=2
    ).astype(jnp.int32)
    line = lax.broadcasted_iota(jnp.int32, (4, hi_size), 0)
    table = jnp.where(
        line == 0,
        qbase,
        jnp.where(
            line == 1,
            starts[:, 0] // KEYS,
            jnp.where(line == 2, (qbase + TILE - 1) // KEYS + 1, core * TILE),
        ),
    ).astype(jnp.int32)
    starts = starts[:, None, :]

    small = [b_query, b_value, g_attn, c_attn, b_out, g_inner, c_inner, g_ffn, c_ffn, b_down]
    large = [b_up, g_mid, c_mid]
    narrow, broad = stacked(small), stacked(large)
    narrow = in_order(wsh, narrow, swap(narrow, "wsh"), axis=1).astype(F32)
    broad = in_order(wsh, broad, swap(broad, "wsh"), axis=1).astype(F32)
    (bq, bv, ga, ca, bo, gi, ci, gf, cf, bd) = [narrow[i] for i in range(10)]
    (bu, gm, cm) = [broad[i] for i in range(3)]

    def whole_weight(weight, after):
        if after is not None:
            weight, _ = lax.optimization_barrier((weight, after))
        half = weight.shape[0] // 2
        sent = lax.dynamic_slice_in_dim(weight, core * half, half, 0)
        first = swap(sent, "wsh")
        second = swap(first, "core")
        return in_order(wsh, weight, in_order(core, first, second)), first

    qkv_full, mark = whole_weight(w_qkv, None)
    out_full, mark = whole_weight(w_out, mark)
    up_full, mark = whole_weight(w_up, mark)
    down_full, mark = whole_weight(w_down, mark)
    cot_pair = swap(lax.optimization_barrier((cotangent, mark))[0], "wsh")

    inputs = tokens.astype(F32)
    normed_attn, back_attn = jax.vjp(layer_norm, inputs, ga, ca)
    attn_low = normed_attn.astype(BF)
    attn_rows = lax.all_gather(attn_low, CHIPS, axis=0, tiled=True)
    projected = jnp.dot(attn_low, qkv_full, preferred_element_type=F32)
    query_low = (projected[:, :feature] + bq).astype(BF)
    key_low = projected[:, feature : 2 * feature].astype(BF)
    value_low = (projected[:, 2 * feature :] + bv).astype(BF)

    def side_by_side(value):
        split = value.reshape(2, HD, HEADS, HD)
        return jnp.transpose(split, (2, 1, 0, 3)).reshape(HEADS, HD, BLK)

    def back_to_rows(value):
        split = value.reshape(HEADS, HD, 2, HD)
        return jnp.transpose(split, (2, 1, 0, 3)).reshape(rows, feature)

    def to_heads(value):
        padded = jnp.pad(value, ((0, chips - HEADS), (0, 0), (0, 0)))
        return lax.all_to_all(padded, CHIPS, 0, 0, tiled=True)

    def to_tokens(value):
        return lax.all_to_all(value, CHIPS, 0, 0, tiled=True)[:HEADS]

    kv_low = jnp.concatenate(
        [key_low.reshape(rows, HEADS, HD), value_low.reshape(rows, HEADS, HD)], axis=2
    )
    kv_low = jnp.transpose(kv_low, (1, 0, 2))
    message = to_heads(jnp.concatenate([kv_low, side_by_side(query_low)], axis=1))
    kv_mine = message[:, :BLK].reshape(hi_size, TILE, BLK)
    queries = message[:, BLK:].reshape(hi_size, 2, HD, BLK)
    kv_other = swap(kv_mine, "core")
    packed, out_t, lse, turned = attend_forward(table, queries, kv_mine, kv_other, starts)
    attended = back_to_rows(to_tokens(packed.reshape(chips, HD, BLK))).astype(F32)

    normed_inner, back_inner = jax.vjp(layer_norm, attended, gi, ci)
    inner_low = normed_inner.astype(BF)
    middle = inputs + jnp.dot(inner_low, out_full, preferred_element_type=F32) + bo
    blocks = jnp.arange(deal_order.shape[0], dtype=jnp.int32)
    given = jnp.sum(jnp.where(deal_order[None, :] == blocks[:, None], blocks[None, :], 0), axis=1)
    picked = jnp.take(lse.reshape(chips, BLK), (given // 4) * 2 + given % 2, axis=0)
    picked = jnp.where(((given // 2) % 2 == core)[:, None], picked, 0.0)
    picked, _ = lax.optimization_barrier((picked, middle))
    lse_got = lax.all_to_all(picked[:, None, :], ALL, 0, 0, tiled=True)
    lse_got = lse_got.reshape(hi_size, 2, 2, BLK)
    lse_slots = (lse_got[:, 0] + lse_got[:, 1]).reshape(chips, BLK)[:HEADS]

    normed_ffn, back_ffn = jax.vjp(layer_norm, middle, gf, cf)
    ffn_low = normed_ffn.astype(BF)
    pre_act = jnp.dot(ffn_low, up_full, preferred_element_type=F32) + bu
    activated, back_gelu = jax.vjp(partial(jax.nn.gelu, approximate=False), pre_act)
    normed_mid, back_mid = jax.vjp(layer_norm, activated, gm, cm)
    mid_low = normed_mid.astype(BF)
    layer_low = (middle + jnp.dot(mid_low, down_full, preferred_element_type=F32) + bd).astype(BF)

    d_out_f = cotangent.astype(F32)
    grad_bd = jnp.sum(d_out_f, axis=0)
    d_mid, grad_gm, grad_cm = back_mid(
        jnp.einsum("tj,ij->ti", cotangent, down_full, preferred_element_type=F32)
    )
    d_pre = back_gelu(d_mid)[0].astype(BF)
    grad_bu = jnp.sum(d_pre.astype(F32), axis=0)
    d_ffn, grad_gf, grad_cf = back_ffn(
        jnp.einsum("tj,ij->ti", d_pre, up_full, preferred_element_type=F32)
    )
    d_middle = d_out_f + d_ffn
    d_branch = d_middle.astype(BF)
    grad_bo = jnp.sum(d_branch.astype(F32), axis=0)
    d_att, grad_gi, grad_ci = back_inner(
        jnp.einsum("tj,ij->ti", d_branch, out_full, preferred_element_type=F32)
    )
    d_att_low = d_att.astype(BF)

    def halves(value):
        size = value.shape[1] // 2
        mine = lax.dynamic_slice_in_dim(value, wsh * size, size, 1)
        other = lax.dynamic_slice_in_dim(value, (1 - wsh) * size, size, 1)
        return mine, other

    def weight_grad(mine, got, right, right_got):
        left = jnp.concatenate([mine, got], axis=0)
        return jnp.einsum(
            "ti,tj->ij", left, jnp.concatenate([right, right_got], axis=0),
            preferred_element_type=F32,
        ).astype(BF)

    mid_mine, mid_other = halves(mid_low)
    ffn_mine, ffn_other = halves(ffn_low)
    inner_mine, inner_other = halves(inner_low)
    mid_got = swap(mid_other, "wsh")
    ffn_got = swap(ffn_other, "wsh")
    inner_got = swap(inner_other, "wsh")
    pre_got = swap(d_pre, "wsh")
    branch_got = swap(d_branch, "wsh")
    grad_down = weight_grad(mid_mine, mid_got, cotangent, cot_pair)
    grad_up = weight_grad(ffn_mine, ffn_got, d_pre, pre_got)
    grad_out = weight_grad(inner_mine, inner_got, d_branch, branch_got)
    t_down, t_up, t_out = (
        total.astype(F32)
        for total in lax.psum((grad_down, grad_up, grad_out), ("hi", "core"))
    )

    douts = to_heads(side_by_side(d_att_low)).reshape(hi_size, 2, HD, BLK)
    douts, _ = lax.optimization_barrier((douts, (grad_down, grad_up, grad_out)))
    dq_packed, dq_wide, dkv_mine, dkv_other = attend_backward(
        table, queries, douts, kv_mine, kv_other, turned, starts, out_t, lse
    )
    dkv_sum = (dkv_mine.astype(F32) + swap(dkv_other, "core").astype(F32)).astype(BF)
    message = to_tokens(
        jnp.concatenate(
            [dkv_sum.reshape(chips, BLK, BLK), dq_packed.reshape(chips, HD, BLK)], axis=1
        )
    )

    def head_grad(right):
        return jnp.einsum(
            "ti,tj->ij", attn_rows, right.reshape(-1, BLK), preferred_element_type=F32
        )

    head = jnp.concatenate([head_grad(dq_wide), head_grad(dkv_sum)], axis=1).astype(BF)
    quarter = feature // 4
    head = head.reshape(2, 2, quarter, 2 * BLK)
    head_kept = lax.dynamic_index_in_dim(head, core, 1, keepdims=False)
    head_sent = lax.dynamic_index_in_dim(head, 1 - core, 1, keepdims=False)
    head = (head_kept.astype(F32) + swap(head_sent, "core").astype(F32)).astype(BF)
    head_kept = lax.dynamic_index_in_dim(head, wsh, 0, keepdims=False)
    head_sent = lax.dynamic_index_in_dim(head, 1 - wsh, 0, keepdims=False)
    head_got = swap(head_sent, "wsh")
    pieces = [
        in_order(wsh, head_kept[:, at : at + HD], head_got[:, at : at + HD], axis=1)
        for at in (0, BLK, BLK + HD)
    ]
    part = gather_steps(jnp.stack(pieces)[None], plain, sizes, index)
    levels = len(bits)
    part = part.reshape((2,) * (levels + 1) + (3, quarter, BLK))
    order = (0, levels + 2, levels + 1) + tuple(range(levels, 0, -1)) + (levels + 3,)
    part = jnp.transpose(part, order).reshape(2 * quarter, 3, hi_size, BLK)
    t_qkv = part[:, :, : HEADS // 2].reshape(2 * quarter, 3 * feature).astype(F32)

    def head_sums(value):
        sums = jnp.sum(value.reshape(-1, BLK).astype(F32), axis=0)
        row = lax.broadcasted_iota(jnp.int32, (HEADS, HD), 0)
        return row == hi * 2 + wsh, sums

    own, sums_q = head_sums(dq_wide)
    own, sums_kv = head_sums(dkv_sum)
    grad_bq = jnp.where(own, sums_q[None, :HD], 0.0).reshape(feature)
    grad_bv = jnp.where(own, sums_kv[None, HD:], 0.0).reshape(feature)

    dq_low = back_to_rows(message[:, BLK:])
    dkv_rows = jnp.transpose(message[:, :BLK], (1, 0, 2)).reshape(rows, HEADS, 2, HD)
    dk_low = dkv_rows[:, :, 0].reshape(rows, feature)
    dv_low = dkv_rows[:, :, 1].reshape(rows, feature)
    d_qkv = jnp.concatenate([dq_low, dk_low, dv_low], axis=1)
    d_input, grad_ga, grad_ca = back_attn(
        jnp.einsum("tj,ij->ti", d_qkv, qkv_full, preferred_element_type=F32)
    )
    grad_low = (d_middle + d_input).astype(BF)

    def sum_over_all(value, cut=True):
        for axis, bit, size in [("core", 1, 2), ("wsh", 1, 2)] + [
            ("hi", bit, hi_size) for bit in bits
        ]:
            value = value + lax.ppermute(value, axis, partner(axis, bit, size))
        return halves(value)[0] if cut else value

    late = sum_over_all(stacked([grad_bq, grad_bv, grad_ga, grad_ca]))
    broad = stacked([grad_bu, grad_gm, grad_cm]).reshape(3, 2, 2, feature)
    early = stacked([grad_bo, grad_gi, grad_ci, grad_gf, grad_cf, grad_bd])
    early = sum_over_all(jnp.concatenate([early, broad.reshape(12, feature)]), False)
    broad = lax.dynamic_index_in_dim(early[6:].reshape(3, 2, 2, feature), wsh, 1, False)
    early = halves(early[:6])[0]
    t_bq, t_bv, t_ga, t_ca = [late[i] for i in range(4)]
    t_bo, t_gi, t_ci, t_gf, t_cf, t_bd = [early[i] for i in range(6)]
    t_bu, t_gm, t_cm = [broad[i].reshape(2 * feature) for i in range(3)]
    return (
        layer_low,
        grad_low,
        lse_slots,
        t_qkv,
        t_bq,
        t_bv,
        t_ga,
        t_ca,
        t_out,
        t_bo,
        t_gi,
        t_ci,
        t_up,
        t_bu,
        t_gf,
        t_cf,
        t_down,
        t_bd,
        t_gm,
        t_cm,
    )


def solution(mesh):
    hi_size = mesh.shape["ctx"] // 2
    inner = Mesh(mesh.devices.reshape(hi_size, 2, mesh.shape["wsh"]), ALL)
    row, mat, vec = P(ALL, None), P("wsh", None), P("wsh")
    grads = (
        mat, vec, vec, vec, vec, mat, vec, vec, vec, mat, vec, vec, vec, mat, vec, vec, vec,
    )
    return jax.shard_map(
        partial(body, hi_size),
        mesh=inner,
        in_specs=(row, P(), P()) + grads + (row,),
        out_specs=(row, row, P(None, ALL)) + grads,
        check_vma=False,
    )
```
